32 devices in a mesh: recv: 4 (over x, core), send: 8 (over z, y).
Axes of the slice: x: 2, y: 2, z: 4, core: 2. Of those that a mesh axis runs over, the one named last changes fastest.
Arguments:
- latent: float32 [4096, 512], P(('recv', 'send')), may hold values from -6 to 6
- edge_feat: float32 [32768, 512], P(('recv', 'send')), may hold values from -6 to 6
- senders: int32 [32768], P(('recv', 'send')), may hold values from 0 to 4095, as said below
- receivers: int32 [32768], P(('recv', 'send')), may hold values from 0 to 4095, as said below
- live_blocks: int32 [32], P(('recv', 'send')), may hold values from 1 to 8, as said below
- cotangent: float32 [32768, 512], P(('recv', 'send')), may hold values from -6 to 6
- w_first: float32 [1536, 512], replicated, may hold values from -0.15625 to 0.15625
- first_bias: float32 [512], replicated, may hold values from -3 to 3
- w_second: float32 [512, 512], replicated, may hold values from -0.25 to 0.25
- second_bias: float32 [512], replicated, may hold values from -3 to 3
- norm_gain: float32 [512], replicated, may hold values from 0.1 to 1.9
Outputs:
- edge_grad: float32 [32768, 512], P(('recv', 'send'))
- sender_grad: float32 [4096, 512], P(('recv', 'send'))
- receiver_grad: float32 [4096, 512], P(('recv', 'send'))
- first_weight_grad: float32 [1536, 512], replicated
- second_weight_grad: float32 [512, 512], replicated
- bias_grads: float32 [4, 512], replicated
The draws below stay inside these ranges and needn't reach their ends.
Inputs may be any that keep to these rules, and one draw needn't show every extreme that they name: `receivers`: slot e lies in tile t = e // 1024; with i = t // (devices along send), its receiver r has (r // 128) // (devices along send) = i. The first two slots of every tile name the last and the first node of that receiver block. `senders`: slot e lies in tile t = e // 1024; with j = t mod (devices along send), its sender s has (s // 128) mod (devices along send) = j. The first two slots of every tile name the last and the first node of that sender block. Tile t's first 128 * live_blocks[t] slots hold edges; its other slots are padding whose cotangent is ignored. Some tile is full in every draw.
All inputs are finite; a program needn't handle non-finite values.
Results may differ from the reference program's by a relative error of at most 0.0001.
Values sent between devices are 32-bit elements; how exact they have to be, the bound alone decides.
A program may use at most 128 MiB of HBM per device.

```python
import math
import jax
import jax.numpy as jnp
from jax import lax

D = 512
NODE_DEV = 128
EDGE_DEV = 1024
CAP_BLOCKS = 8
NODES = 4096
EDGES = 32768
N_RECV = 4
N_SEND = 8


def slot_layout():
    slot_total = EDGE_DEV * N_RECV * N_SEND
    slot = jnp.arange(slot_total, dtype=jnp.int32)
    tile = slot // EDGE_DEV
    return (slot_total, tile // N_SEND, tile % N_SEND, slot % EDGE_DEV)


def draw_receivers(key, part):
    slot_total, row_block, col_block, position = slot_layout()
    keys = jax.random.split(jax.random.fold_in(key, 11), 2)
    column = jax.random.randint(keys[0], (slot_total,), 0, N_SEND)
    within = jax.random.randint(keys[1], (slot_total,), 0, NODE_DEV)
    ids = (row_block * N_SEND + column) * NODE_DEV + within
    ids = jnp.where(position == 0, (row_block * N_SEND + N_SEND - 1) * NODE_DEV + NODE_DEV - 1, ids)
    ids = jnp.where(position == 1, row_block * N_SEND * NODE_DEV, ids)
    return ids.astype(jnp.int32)


def draw_senders(key, part):
    slot_total, row_block, col_block, position = slot_layout()
    keys = jax.random.split(jax.random.fold_in(key, 23), 2)
    band = jax.random.randint(keys[0], (slot_total,), 0, N_RECV)
    within = jax.random.randint(keys[1], (slot_total,), 0, NODE_DEV)
    ids = (band * N_SEND + col_block) * NODE_DEV + within
    ids = jnp.where(position == 0, ((N_RECV - 1) * N_SEND + col_block) * NODE_DEV + NODE_DEV - 1, ids)
    ids = jnp.where(position == 1, col_block * NODE_DEV, ids)
    return ids.astype(jnp.int32)


def draw_live_blocks(key, part):
    tile_total = N_RECV * N_SEND
    keys = jax.random.split(jax.random.fold_in(key, 37), 3)
    base = jax.random.randint(keys[0], (tile_total,), 1, 3)
    heavy = jax.random.randint(keys[1], (tile_total,), 0, 4) == 0
    counts = jnp.where(heavy, CAP_BLOCKS, base)
    forced = jax.random.randint(keys[2], (), 0, tile_total)
    counts = jnp.where(jnp.arange(tile_total, dtype=jnp.int32) == forced, CAP_BLOCKS, counts)
    return jnp.minimum(counts, CAP_BLOCKS).astype(jnp.int32)


def shard_levels(stream_key, dims, shards, least, largest):
    level = 1.0
    for axis_at, shards_of in shards:
        steps = jax.random.uniform(jax.random.fold_in(jax.random.fold_in(stream_key, 6), axis_at), (shards_of,), jnp.float32, least / len(shards), largest / len(shards))
        level = level * jnp.repeat(jnp.exp(steps), dims[axis_at] // shards_of).reshape((-1,) + (1,) * (len(dims) - 1 - axis_at))
    return level


def bell_draw(rng, extent, spread, limit, shards=(), kind=jnp.bfloat16):
    level = shard_levels(rng, extent, shards, -0.22, 0.18) if shards else 1.0
    entries = jax.random.normal(rng, extent, jnp.float32) * spread * level
    return jnp.minimum(jnp.maximum(entries, -limit), limit).astype(kind)


def setup_inputs(seed: int = 0) -> dict:
    streams_of = jax.random.split(jax.random.key(seed), 12)
    return {
        "latent": bell_draw(streams_of[0], (NODES, D), 1.0, 6.0, ((0, 32),), jnp.float32),
        "edge_feat": bell_draw(streams_of[1], (EDGES, D), 1.0, 6.0, ((0, 32),), jnp.float32),
        "senders": draw_senders(jax.random.fold_in(streams_of[11], 71), 0),
        "receivers": draw_receivers(jax.random.fold_in(streams_of[11], 71), 0),
        "live_blocks": draw_live_blocks(jax.random.fold_in(streams_of[11], 71), 0),
        "cotangent": bell_draw(streams_of[5], (EDGES, D), 1.0, 6.0, ((0, 32),), jnp.float32),
        "w_first": bell_draw(streams_of[6], (3 * D, D), (3 * D) ** -0.5, 0.15625, (), jnp.float32),
        "first_bias": bell_draw(streams_of[7], (D,), 0.5, 3.0, (), jnp.float32),
        "w_second": bell_draw(streams_of[8], (D, D), D ** -0.5, 0.25, (), jnp.float32),
        "second_bias": bell_draw(streams_of[9], (D,), 0.5, 3.0, (), jnp.float32),
        "norm_gain": jnp.clip(1.0 + 0.18 * jax.random.normal(streams_of[10], (D,), jnp.float32), 0.1, 1.9),
    }


def layer_forward(edge_rows, sender_rows, receiver_rows, w_first, first_bias, w_second, second_bias, norm_gain):
    joined = jnp.concatenate([edge_rows, sender_rows, receiver_rows], axis=1)
    hidden = jnp.dot(joined, w_first, precision=lax.Precision.HIGHEST) + first_bias
    active = jax.nn.silu(hidden)
    output = jnp.dot(active, w_second, precision=lax.Precision.HIGHEST) + second_bias
    centred = output - lax.optimization_barrier(jnp.mean(output, axis=1, keepdims=True))
    variance = lax.optimization_barrier(jnp.mean(centred * centred, axis=1, keepdims=True))
    return centred * lax.rsqrt(variance + 1e-05) * norm_gain

def reference(latent, edge_feat, senders, receivers, live_blocks, cotangent, w_first, first_bias, w_second, second_bias, norm_gain):
    tile_count = N_RECV * N_SEND
    model_width = latent.shape[1]
    position = jnp.arange(EDGE_DEV, dtype=jnp.int32)
    live_mask = (position[None, :] < 128 * live_blocks[:, None]).astype(jnp.float32)
    tiles_edge = edge_feat.reshape(tile_count, EDGE_DEV, model_width)
    tiles_grad = cotangent.reshape(tile_count, EDGE_DEV, model_width) * live_mask[:, :, None]
    tiles_send = senders.reshape(tile_count, EDGE_DEV).astype(jnp.int32)
    tiles_recv = receivers.reshape(tile_count, EDGE_DEV).astype(jnp.int32)

    def one_tile(state, inputs):
        first_grad, second_grad, small_grad, sender_grad, receiver_grad = state
        edge_rows, grad_rows, send_ids, recv_ids = inputs
        sender_rows = jnp.take(latent, send_ids, axis=0)
        receiver_rows = jnp.take(latent, recv_ids, axis=0)
        normed, pullback = jax.vjp(layer_forward, edge_rows, sender_rows, receiver_rows, w_first, first_bias, w_second, second_bias, norm_gain)
        grad_edge, grad_send, grad_recv, grad_first, grad_fbias, grad_second, grad_sbias, grad_gain = pullback(grad_rows)
        small = jnp.stack([grad_fbias, grad_sbias, grad_gain, lax.optimization_barrier(jnp.sum(grad_rows, axis=0))])
        sender_grad = sender_grad.at[send_ids].add(grad_send)
        receiver_grad = receiver_grad.at[recv_ids].add(grad_recv)
        state = (first_grad + grad_first, second_grad + grad_second, small_grad + small, sender_grad, receiver_grad)
        return (state, grad_rows + grad_edge)
    initial = (jnp.zeros(w_first.shape, jnp.float32), jnp.zeros(w_second.shape, jnp.float32), jnp.zeros((4, model_width), jnp.float32), jnp.zeros(latent.shape, jnp.float32), jnp.zeros(latent.shape, jnp.float32))
    state, edge_tiles = lax.scan(one_tile, initial, (tiles_edge, tiles_grad, tiles_send, tiles_recv))
    first_grad, second_grad, small_grad, sender_grad, receiver_grad = state
    factor = 1.0 / math.sqrt(EDGES)
    edge_grad = edge_tiles.reshape(tile_count * EDGE_DEV, model_width)
    return (edge_grad, sender_grad, receiver_grad, first_grad * factor, second_grad * factor, small_grad * factor)
```

```python
import functools
import math

import jax
import jax.numpy as jnp
from jax import lax
from jax.experimental import pallas as pl
from jax.experimental.pallas import tpu as pltpu
from jax.sharding import PartitionSpec as P

norm_eps = 1e-05
block_rows = 128
step_rows = 256
MESH = pl.DeviceIdType.MESH
NN = (((1,), (0,)), ((), ()))
NT = (((1,), (1,)), ((), ()))
TN = (((0,), (0,)), ((), ()))


def split(value):
    high = value.astype(jnp.bfloat16)
    low = (value - high.astype(jnp.float32)).astype(jnp.bfloat16)
    return high, low


def mm(left, right, dims):
    return lax.dot_general(left, right, dims, preferred_element_type=jnp.float32)


def dot3(left, right, dims):
    return mm(left[0], right[0], dims) + mm(left[0], right[1], dims) + mm(left[1], right[0], dims)


def dot2(exact, right):
    return mm(exact, right[0], NN) + mm(exact, right[1], NN)


def bits_of(count):
    return max(count.bit_length() - 1, 0)


def my_bit(axis, bit):
    return (lax.axis_index(axis) // (1 << bit)) % 2


def partner_of(axis, bit):
    mine = my_bit(axis, bit)
    other = lax.axis_index(axis) + (1 - 2 * mine) * (1 << bit)
    if axis == "recv":
        return (other, lax.axis_index("send"))
    return (lax.axis_index("recv"), other)


def greet(moves):
    barrier = pltpu.get_barrier_semaphore()
    for axis, bit in moves:
        pl.semaphore_signal(barrier, inc=1, device_id=partner_of(axis, bit), device_id_type=MESH)
    pl.semaphore_wait(barrier, len(moves))


def run_streams(streams):
    live = list(streams)
    while live:
        after = []
        for stream in live:
            try:
                next(stream)
                after.append(stream)
            except StopIteration:
                pass
        live = after


def send_to(src, dst, sems, at, axis, bit):
    copy = pltpu.make_async_remote_copy(
        src_ref=src,
        dst_ref=dst,
        send_sem=sems.at[0, at],
        recv_sem=sems.at[1, at],
        device_id=partner_of(axis, bit),
        device_id_type=MESH,
    )
    copy.start()
    return copy


def gather_stream(table, sems, base, axis, order, cols):
    count = len(order)
    done = set()
    for at, bit in enumerate(order):
        index = []
        for dim in range(count):
            owner = count - 1 - dim
            index.append(pl.ds(0, 2) if owner in done else pl.ds(my_bit(axis, owner), 1))
        region = table.at[tuple(index) + (slice(None), cols)]
        copy = send_to(region, region, sems, base + at, axis, bit)
        yield
        copy.wait()
        done.add(bit)


def gather_kernel(plan, latent_ref, ts_ref, tr_ref, sems):
    for table, axis in ((ts_ref, "recv"), (tr_ref, "send")):
        count = table.ndim - 2
        at = tuple(my_bit(axis, count - 1 - dim) for dim in range(count))
        table[at] = latent_ref[...]
    greet(plan["moves"])
    streams = []
    base = 0
    for axis, order, cols in plan["gather"]:
        table = ts_ref if axis == "recv" else tr_ref
        streams.append(gather_stream(table, sems, base, axis, order, pl.ds(*cols)))
        base += len(order)
    run_streams(streams)


def add_rows(dst, left, right, rows):
    chunk = min(rows, 64)

    def body(i, carry):
        at = pl.ds(pl.multiple_of(i * chunk, chunk), chunk)
        dst[at, :] = left[at, :] + right[at, :]
        return carry

    lax.fori_loop(0, rows // chunk, body, 0)


def scatter_stream(source, slots, sems, base, axis, order, cols, out, width):
    held = source
    left = sorted(order, reverse=True)
    for at, bit in enumerate(order):
        place = left.index(bit)
        mine = my_bit(axis, bit)
        pick = lambda ref, which: ref.at[(slice(None),) * place + (which,)]
        if at == 0:
            outgoing = source.at[(slice(None),) * place + (1 - mine,) + (slice(None),) * (len(left) - place) + (cols,)]
            kept = source.at[(slice(None),) * place + (mine,) + (slice(None),) * (len(left) - place) + (cols,)]
        else:
            outgoing, kept = pick(held, 1 - mine), pick(held, mine)
        slot = slots[at]
        copy = send_to(outgoing, slot, sems, base + at, axis, bit)
        yield
        copy.wait()
        left.remove(bit)
        lead = 1 << len(left)
        for piece in range(lead):
            at_piece = tuple((piece >> (len(left) - 1 - d)) & 1 for d in range(len(left)))
            target = out.at[:, cols] if not left else slot.at[at_piece]
            first = slot.at[at_piece] if left else slot
            second = kept.at[at_piece] if left else kept
            add_rows(target, first, second, block_rows)
        held = slot


def total_stream(source, slots, sems, base, order, cols, out, factor):
    rows = source.shape[0]
    held, offset = source.at[:, cols], 0
    trail = []
    for at, (axis, bit) in enumerate(order):
        rows //= 2
        mine = my_bit(axis, bit)
        slot = slots[at]
        outgoing = held.at[pl.ds(pl.multiple_of((1 - mine) * rows, rows), rows)]
        kept = held.at[pl.ds(pl.multiple_of(mine * rows, rows), rows)]
        copy = send_to(outgoing, slot, sems, base + at, axis, bit)
        yield
        copy.wait()
        add_rows(slot, slot, kept, rows)
        held = slot
        offset = offset + mine * rows
        trail.append((axis, bit, rows, offset))
    out[pl.ds(pl.multiple_of(offset, rows), rows), cols] = held[...] * factor
    base += len(order)
    for at, (axis, bit, rows, offset) in enumerate(reversed(trail)):
        region = out.at[pl.ds(pl.multiple_of(offset, rows), rows), cols]
        copy = send_to(region, region, sems, base + at, axis, bit)
        yield
        copy.wait()


def small_stream(source, slots, sems, base, order, out, factor):
    out[...] = source[...]
    for at, (axis, bit) in enumerate(order):
        held = source if at == 0 else slots.at[2 * at - 1]
        copy = send_to(held, slots.at[2 * at], sems, base + at, axis, bit)
        yield
        copy.wait()
        slots[2 * at + 1] = held[...] + slots[2 * at]
    out[...] = slots[2 * len(order) - 1] * factor


def reduce_kernel(plan, factor, s_ref, r_ref, g_ref, small_ref, s_out, r_out, g_out, small_out, sems, small_slots, *slots):
    greet(plan["moves"])
    streams = []
    base = 0
    used = 0
    for axis, order, cols in plan["scatter"]:
        source, out = (s_ref, s_out) if axis == "recv" else (r_ref, r_out)
        streams.append(
            scatter_stream(source, slots[used : used + len(order)], sems, base, axis, order, pl.ds(*cols), out, cols[1])
        )
        base += len(order)
        used += len(order)
    for order, cols in plan["total"]:
        streams.append(
            total_stream(g_ref, slots[used : used + len(order)], sems, base, order, pl.ds(*cols), g_out, factor)
        )
        base += 2 * len(order)
        used += len(order)
    streams.append(small_stream(small_ref, small_slots, sems, base, plan["moves"], small_out, factor))
    run_streams(streams)


def edge_kernel(
    live_ref,
    edge_ref,
    cot_ref,
    scol_ref,
    srow_ref,
    rcol_ref,
    rrow_ref,
    ts_ref,
    tr_ref,
    w1_ref,
    b1_ref,
    w2_ref,
    b2_ref,
    gain_ref,
    edge_out,
    s_out,
    r_out,
    g_out,
    small_out,
    w1h,
    w1l,
    w2h,
    w2l,
    psh,
    psl,
    prh,
    prl,
):
    width = w2_ref.shape[0]
    send_nodes, recv_nodes = ts_ref.shape[0], tr_ref.shape[0]
    slots = edge_ref.shape[0]
    live_limit = block_rows * live_ref[0]

    def rows_at(i, rows=step_rows):
        return pl.ds(pl.multiple_of(i * rows, rows), rows)

    def split_first(i, carry):
        at = rows_at(i)
        w1h[at, :], w1l[at, :] = split(w1_ref[at, :])
        return carry

    def split_second(i, carry):
        at = rows_at(i)
        w2h[at, :], w2l[at, :] = split(w2_ref[at, :])
        return carry

    lax.fori_loop(0, 3 * width // step_rows, split_first, 0)
    lax.fori_loop(0, width // step_rows, split_second, 0)
    part = [pl.ds(k * width, width) for k in range(3)]

    def project(table, high, low, rows):
        def body(i, carry):
            at = rows_at(i)
            value = dot3(split(table[at, :]), (w1h[rows, :], w1l[rows, :]), NN)
            high[at, :], low[at, :] = split(value)
            return carry

        lax.fori_loop(0, table.shape[0] // step_rows, body, 0)

    project(ts_ref, psh, psl, part[1])
    project(tr_ref, prh, prl, part[2])
    s_out[...] = jnp.zeros_like(s_out)
    r_out[...] = jnp.zeros_like(r_out)
    g_out[...] = jnp.zeros_like(g_out)
    small_out[...] = jnp.zeros_like(small_out)

    def step(i, carry):
        at = rows_at(i)
        edge_rows = edge_ref[at, :]
        edge_parts = split(edge_rows)
        position = i * step_rows + lax.broadcasted_iota(jnp.int32, (step_rows, 1), 0)
        grad_rows = cot_ref[at, :] * (position < live_limit).astype(jnp.float32)

        def pick(col, nodes):
            lane = lax.broadcasted_iota(jnp.int32, (step_rows, nodes), 1)
            return (col[at, :] == lane).astype(jnp.float32).astype(jnp.bfloat16)

        def spread(row, nodes):
            line = lax.broadcasted_iota(jnp.int32, (nodes, step_rows), 0)
            return (row[:, at] == line).astype(jnp.float32).astype(jnp.bfloat16)

        hidden = dot3(edge_parts, (w1h[part[0], :], w1l[part[0], :]), NN)
        hidden = hidden + dot2(pick(scol_ref, send_nodes), (psh[...], psl[...]))
        hidden = hidden + dot2(pick(rcol_ref, recv_nodes), (prh[...], prl[...]))
        hidden = hidden + b1_ref[...]
        sigmoid_hidden = jax.nn.sigmoid(hidden)
        active = split(hidden * sigmoid_hidden)
        second = (w2h[...], w2l[...])
        output = dot3(active, second, NN) + b2_ref[...]
        centred = output - jnp.mean(output, axis=1, keepdims=True)
        inv_std = lax.rsqrt(jnp.mean(centred * centred, axis=1, keepdims=True) + norm_eps)
        normed = centred * inv_std
        scaled = grad_rows * gain_ref[...]
        norm_grad = inv_std * (
            scaled
            - jnp.mean(scaled, axis=1, keepdims=True)
            - normed * jnp.mean(scaled * normed, axis=1, keepdims=True)
        )
        norm_parts = split(norm_grad)
        hidden_grad = dot3(norm_parts, second, NT) * sigmoid_hidden * (1.0 + hidden * (1.0 - sigmoid_hidden))
        hidden_parts = split(hidden_grad)
        edge_out[at, :] = grad_rows + dot3(hidden_parts, (w1h[part[0], :], w1l[part[0], :]), NT)
        g_out[part[0], :] += dot3(edge_parts, hidden_parts, TN)
        g_out[pl.ds(3 * width, width), :] += dot3(active, norm_parts, TN)
        small_out[0:1, :] += jnp.sum(hidden_grad, axis=0, keepdims=True)
        small_out[1:2, :] += jnp.sum(norm_grad, axis=0, keepdims=True)
        small_out[2:3, :] += jnp.sum(grad_rows * normed, axis=0, keepdims=True)
        small_out[3:4, :] += jnp.sum(grad_rows, axis=0, keepdims=True)
        s_out[...] += dot2(spread(srow_ref, send_nodes), hidden_parts)
        r_out[...] += dot2(spread(rrow_ref, recv_nodes), hidden_parts)
        return carry

    steps = (live_limit + step_rows - 1) // step_rows
    lax.fori_loop(0, steps, step, 0)

    def blank(i, carry):
        edge_out[rows_at(i), :] = jnp.zeros((step_rows, width), jnp.float32)
        return carry

    lax.fori_loop(steps, slots // step_rows, blank, 0)

    def outer(table, sums, rows):
        def body(i, carry):
            at = rows_at(i)
            g_out[rows, :] += dot3(split(table[at, :]), split(sums[at, :]), TN)
            return carry

        lax.fori_loop(0, table.shape[0] // step_rows, body, 0)

    outer(ts_ref, s_out, part[1])
    outer(tr_ref, r_out, part[2])


def f32(*shape):
    return jax.ShapeDtypeStruct(shape, jnp.float32)


def make_plan(recv_bits, send_bits, width):
    half = width // 2
    recv_up = list(range(recv_bits))
    send_up = list(range(send_bits))
    recv_down, send_down = recv_up[::-1], send_up[::-1]
    recv_moves = [("recv", bit) for bit in recv_up]
    send_moves = [("send", bit) for bit in send_up]
    late_first = send_up[1:] + send_up[:1]
    return {
        "moves": recv_moves + send_moves,
        "gather": [
            ("recv", recv_down, (0, width)),
            ("send", send_down, (0, half)),
            ("send", send_up[:1] + send_down[:-1], (half, half)),
        ],
        "scatter": [
            ("recv", recv_up, (0, width)),
            ("send", send_up, (0, half)),
            ("send", late_first, (half, half)),
        ],
        "total": [
            (recv_moves + send_moves, (0, half)),
            (recv_moves[:1] + send_moves + recv_moves[1:], (half, half)),
        ],
    }


def shards(
    latent,
    edge_feat,
    senders,
    receivers,
    live_blocks,
    cotangent,
    w_first,
    first_bias,
    w_second,
    second_bias,
    norm_gain,
):
    node_rows, width = latent.shape
    slot_count = edge_feat.shape[0]
    recv_count = lax.axis_size("recv")
    send_count = lax.axis_size("send")
    recv_bits, send_bits = bits_of(recv_count), bits_of(send_count)
    recv_index = lax.axis_index("recv")
    recv_local = receivers - recv_index * (send_count * node_rows)
    send_local = senders // node_rows // send_count * node_rows + senders % node_rows
    plan = make_plan(recv_bits, send_bits, width)
    factor = 1.0 / math.sqrt(slot_count * recv_count * send_count)
    vmem = pl.BlockSpec(memory_space=pltpu.VMEM)
    recv_shape = (2,) * recv_bits + (node_rows, width)
    send_shape = (2,) * send_bits + (node_rows, width)

    copies = sum(len(order) for _, order, _ in plan["gather"])
    send_table, recv_table = pl.pallas_call(
        functools.partial(gather_kernel, plan),
        out_shape=(f32(*recv_shape), f32(*send_shape)),
        in_specs=[vmem],
        out_specs=(vmem, vmem),
        scratch_shapes=[pltpu.SemaphoreType.DMA((2, copies))],
        compiler_params=pltpu.CompilerParams(collective_id=0, has_side_effects=True, vmem_limit_bytes=40 << 20),
        name="gather_nodes",
    )(latent)
    send_table = send_table.reshape(recv_count * node_rows, width)
    recv_table = recv_table.reshape(send_count * node_rows, width)

    smem = pl.BlockSpec(memory_space=pltpu.SMEM)
    send_nodes, recv_nodes = send_table.shape[0], recv_table.shape[0]
    half_type = jnp.bfloat16
    edge_out, send_sum, recv_sum, weights, small = pl.pallas_call(
        edge_kernel,
        out_shape=(
            f32(slot_count, width),
            f32(send_nodes, width),
            f32(recv_nodes, width),
            f32(4 * width, width),
            f32(8, width),
        ),
        in_specs=[smem] + [vmem] * 13,
        out_specs=(vmem,) * 5,
        scratch_shapes=[
            pltpu.VMEM((3 * width, width), half_type),
            pltpu.VMEM((3 * width, width), half_type),
            pltpu.VMEM((width, width), half_type),
            pltpu.VMEM((width, width), half_type),
            pltpu.VMEM((send_nodes, width), half_type),
            pltpu.VMEM((send_nodes, width), half_type),
            pltpu.VMEM((recv_nodes, width), half_type),
            pltpu.VMEM((recv_nodes, width), half_type),
        ],
        compiler_params=pltpu.CompilerParams(vmem_limit_bytes=60 << 20),
        name="edge_work",
    )(
        live_blocks,
        edge_feat,
        cotangent,
        send_local[:, None],
        send_local[None, :],
        recv_local[:, None],
        recv_local[None, :],
        send_table,
        recv_table,
        w_first,
        first_bias[None, :],
        w_second,
        second_bias[None, :],
        norm_gain[None, :],
    )

    slots = []
    copies = 0
    for _, order, cols in plan["scatter"]:
        for at in range(len(order)):
            slots.append(pltpu.VMEM((2,) * (len(order) - 1 - at) + (node_rows, cols[1]), jnp.float32))
        copies += len(order)
    for order, cols in plan["total"]:
        for at in range(len(order)):
            slots.append(pltpu.VMEM((4 * width >> (at + 1), cols[1]), jnp.float32))
        copies += 2 * len(order)
    moves = len(plan["moves"])
    copies += moves
    send_own, recv_own, weight_total, small_total = pl.pallas_call(
        functools.partial(reduce_kernel, plan, factor),
        out_shape=(f32(node_rows, width), f32(node_rows, width), f32(4 * width, width), f32(8, width)),
        in_specs=[vmem] * 4,
        out_specs=(vmem,) * 4,
        scratch_shapes=[
            pltpu.SemaphoreType.DMA((2, copies)),
            pltpu.VMEM((2 * moves, 8, width), jnp.float32),
        ]
        + slots,
        compiler_params=pltpu.CompilerParams(collective_id=1, has_side_effects=True, vmem_limit_bytes=56 << 20),
        name="sum_grads",
    )(send_sum.reshape(recv_shape), recv_sum.reshape(send_shape), weights, small)

    def back(sums, rows):
        return lax.dot_general(
            sums, rows, NT, precision=lax.Precision.HIGHEST, preferred_element_type=jnp.float32
        )

    return (
        edge_out,
        back(send_own, w_first[width : 2 * width]),
        back(recv_own, w_first[2 * width :]),
        weight_total[: 3 * width],
        weight_total[3 * width :],
        small_total[:4],
    )


def solution(mesh):
    return jax.shard_map(
        shards,
        mesh=mesh,
        in_specs=(
            P(("recv", "send"), None),
            P(("recv", "send"), None),
            P(("recv", "send")),
            P(("recv", "send")),
            P(("recv", "send")),
            P(("recv", "send"), None),
            P(),
            P(),
            P(),
            P(),
            P(),
        ),
        out_specs=(
            P(("recv", "send"), None),
            P(("recv", "send"), None),
            P(("recv", "send"), None),
            P(),
            P(),
            P(),
        ),
        check_vma=False,
    )
```

```python
import functools
import math

import jax
import jax.numpy as jnp
from jax import lax
from jax.experimental import pallas as pl
from jax.experimental.pallas import tpu as pltpu
from jax.sharding import PartitionSpec as P

norm_eps = 1e-05
block_rows = 128
step_rows = 256
MESH = pl.DeviceIdType.MESH
NN = (((1,), (0,)), ((), ()))
NT = (((1,), (1,)), ((), ()))
TN = (((0,), (0,)), ((), ()))


def split(value):
    high = value.astype(jnp.bfloat16)
    low = (value - high.astype(jnp.float32)).astype(jnp.bfloat16)
    return high, low


def mm(left, right, dims):
    return lax.dot_general(left, right, dims, preferred_element_type=jnp.float32)


def dot3(left, right, dims):
    return mm(left[0], right[0], dims) + mm(left[0], right[1], dims) + mm(left[1], right[0], dims)


def dot2(exact, right):
    return mm(exact, right[0], NN) + mm(exact, right[1], NN)


def bits_of(count):
    return max(count.bit_length() - 1, 0)


def my_bit(axis, bit):
    return (lax.axis_index(axis) // (1 << bit)) % 2


def partner_of(axis, bit):
    mine = my_bit(axis, bit)
    other = lax.axis_index(axis) + (1 - 2 * mine) * (1 << bit)
    if axis == "recv":
        return (other, lax.axis_index("send"))
    return (lax.axis_index("recv"), other)


def greet(moves):
    barrier = pltpu.get_barrier_semaphore()
    for axis, bit in moves:
        pl.semaphore_signal(barrier, inc=1, device_id=partner_of(axis, bit), device_id_type=MESH)
    pl.semaphore_wait(barrier, len(moves))


def run_streams(streams):
    live = list(streams)
    while live:
        after = []
        for stream in live:
            try:
                next(stream)
                after.append(stream)
            except StopIteration:
                pass
        live = after


def send_to(src, dst, sems, at, axis, bit):
    copy = pltpu.make_async_remote_copy(
        src_ref=src,
        dst_ref=dst,
        send_sem=sems.at[0, at],
        recv_sem=sems.at[1, at],
        device_id=partner_of(axis, bit),
        device_id_type=MESH,
    )
    copy.start()
    return copy


def gather_stream(table, sems, base, axis, order, cols):
    count = len(order)
    done = set()
    for at, bit in enumerate(order):
        index = []
        for dim in range(count):
            owner = count - 1 - dim
            index.append(pl.ds(0, 2) if owner in done else pl.ds(my_bit(axis, owner), 1))
        region = table.at[tuple(index) + (slice(None), cols)]
        copy = send_to(region, region, sems, base + at, axis, bit)
        yield
        copy.wait()
        done.add(bit)


def add_rows(dst, left, right, rows):
    chunk = min(rows, 64)

    def body(i, carry):
        at = pl.ds(pl.multiple_of(i * chunk, chunk), chunk)
        dst[at, :] = left[at, :] + right[at, :]
        return carry

    lax.fori_loop(0, rows // chunk, body, 0)


def scatter_stream(source, slots, sems, base, axis, order, cols, out, width):
    held = source
    left = sorted(order, reverse=True)
    for at, bit in enumerate(order):
        place = left.index(bit)
        mine = my_bit(axis, bit)
        pick = lambda ref, which: ref.at[(slice(None),) * place + (which,)]
        if at == 0:
            outgoing = source.at[(slice(None),) * place + (1 - mine,) + (slice(None),) * (len(left) - place) + (cols,)]
            kept = source.at[(slice(None),) * place + (mine,) + (slice(None),) * (len(left) - place) + (cols,)]
        else:
            outgoing, kept = pick(held, 1 - mine), pick(held, mine)
        slot = slots[at]
        copy = send_to(outgoing, slot, sems, base + at, axis, bit)
        yield
        copy.wait()
        left.remove(bit)
        lead = 1 << len(left)
        for piece in range(lead):
            at_piece = tuple((piece >> (len(left) - 1 - d)) & 1 for d in range(len(left)))
            target = out.at[:, cols] if not left else slot.at[at_piece]
            first = slot.at[at_piece] if left else slot
            second = kept.at[at_piece] if left else kept
            add_rows(target, first, second, block_rows)
        held = slot


def total_stream(source, slots, sems, base, order, start, rows, cols, out, factor):
    held, offset = source.at[pl.ds(start, rows), cols], 0
    trail = []
    for at, (axis, bit) in enumerate(order):
        slot = slots[at]
        if rows > 8:
            rows //= 2
            mine = my_bit(axis, bit)
            outgoing = held.at[pl.ds(pl.multiple_of((1 - mine) * rows, rows), rows)]
            kept = held.at[pl.ds(pl.multiple_of(mine * rows, rows), rows)]
            offset = offset + mine * rows
            trail.append((axis, bit, rows, offset))
        else:
            outgoing = kept = held
        copy = send_to(outgoing, slot, sems, base + at, axis, bit)
        yield
        copy.wait()
        add_rows(slot, slot, kept, rows)
        held = slot
    out[pl.ds(pl.multiple_of(start + offset, 8), rows), cols] = held[...] * factor
    base += len(order)
    for at, (axis, bit, rows, offset) in enumerate(reversed(trail)):
        region = out.at[pl.ds(pl.multiple_of(start + offset, 8), rows), cols]
        copy = send_to(region, region, sems, base + at, axis, bit)
        yield
        copy.wait()


def small_stream(source, slots, sems, base, order, out, factor):
    out[...] = source[...]
    for at, (axis, bit) in enumerate(order):
        held = source if at == 0 else slots.at[2 * at - 1]
        copy = send_to(held, slots.at[2 * at], sems, base + at, axis, bit)
        yield
        copy.wait()
        slots[2 * at + 1] = held[...] + slots[2 * at]
    out[...] = slots[2 * len(order) - 1] * factor


def rows_at(i, rows=step_rows):
    return pl.ds(pl.multiple_of(i * rows, rows), rows)


def loop(count, body):
    def run(i, carry):
        body(i)
        return carry

    lax.fori_loop(0, count, run, 0)


def whole_kernel(
    plan,
    factor,
    live_ref,
    latent_ref,
    edge_hbm,
    cot_hbm,
    scol_ref,
    srow_ref,
    rcol_ref,
    rrow_ref,
    w1_hbm,
    b1_ref,
    w2_hbm,
    b2_ref,
    gain_ref,
    edge_out,
    s_own,
    r_own,
    g_out,
    small_out,
    sems,
    local_sems,
    edge_ref,
    cot_ref,
    wh,
    wl,
    ts_ref,
    tr_ref,
    ps_ref,
    pr_ref,
    g_ref,
    small_ref,
    own_s,
    own_r,
    small_slots,
    *slots,
):
    slot_count, width = edge_ref.shape
    steps = slot_count // step_rows
    live_limit = block_rows * live_ref[0]
    part = [pl.ds(k * width, width) for k in range(4)]
    node_rows = latent_ref.shape[0]
    send_pieces = [tuple((k >> (ts_ref.ndim - 3 - d)) & 1 for d in range(ts_ref.ndim - 2)) for k in range(1 << (ts_ref.ndim - 2))]
    recv_pieces = [tuple((k >> (tr_ref.ndim - 3 - d)) & 1 for d in range(tr_ref.ndim - 2)) for k in range(1 << (tr_ref.ndim - 2))]

    loads = [
        pltpu.make_async_copy(w2_hbm, g_out.at[part[0]], local_sems.at[0]),
        pltpu.make_async_copy(w1_hbm, g_out.at[pl.ds(width, 3 * width)], local_sems.at[1]),
        pltpu.make_async_copy(edge_hbm, edge_ref, local_sems.at[2]),
        pltpu.make_async_copy(cot_hbm, cot_ref, local_sems.at[3]),
    ]
    for load in loads:
        load.start()
    for table, axis in ((ts_ref, "recv"), (tr_ref, "send")):
        count = table.ndim - 2
        at = tuple(my_bit(axis, count - 1 - dim) for dim in range(count))
        table[at] = latent_ref[...]
    greet(plan["moves"])

    streams = []
    base = 0
    for axis, order, cols in plan["gather"]:
        table = ts_ref if axis == "recv" else tr_ref
        streams.append(gather_stream(table, sems, base, axis, order, pl.ds(*cols)))
        base += len(order)

    def prepare():
        yield
        for load in loads:
            load.wait()

        def split_rows(i):
            at = rows_at(i)
            wh[at, :], wl[at, :] = split(g_out[at, :])

        loop(4 * width // step_rows, split_rows)

        def first_part(i):
            at = rows_at(i)
            edge_out[at, :] = dot3(split(edge_ref[at, :]), (wh[part[1], :], wl[part[1], :]), NN) + b1_ref[...]

        loop(steps, first_part)
        yield

    def project(table, pieces, into, rows):
        for k, piece in enumerate(pieces):
            into[piece] = dot3(split(table[piece]), (wh[rows, :], wl[rows, :]), NN)

    run_streams(streams + [prepare()])
    project(ts_ref, send_pieces, ps_ref, part[2])
    project(tr_ref, recv_pieces, pr_ref, part[3])

    small_ref[...] = jnp.zeros_like(small_ref)
    g_ref[part[0], :] = jnp.zeros((width, width), jnp.float32)
    send_nodes, recv_nodes = len(send_pieces) * node_rows, len(recv_pieces) * node_rows

    def step(i):
        at = rows_at(i)
        position = i * step_rows + lax.broadcasted_iota(jnp.int32, (step_rows, 1), 0)
        grad_rows = cot_ref[at, :] * (position < live_limit).astype(jnp.float32)
        cot_ref[at, :] = grad_rows

        def pick(col, nodes):
            lane = lax.broadcasted_iota(jnp.int32, (step_rows, nodes), 1)
            return (col[at, :] == lane).astype(jnp.float32).astype(jnp.bfloat16)

        send_table = split(ps_ref[...].reshape(send_nodes, width))
        recv_table = split(pr_ref[...].reshape(recv_nodes, width))
        hidden = edge_out[at, :] + dot2(pick(scol_ref, send_nodes), send_table)
        hidden = hidden + dot2(pick(rcol_ref, recv_nodes), recv_table)
        sigmoid_hidden = jax.nn.sigmoid(hidden)
        active = split(hidden * sigmoid_hidden)
        second = (wh[part[0], :], wl[part[0], :])
        output = dot3(active, second, NN) + b2_ref[...]
        centred = output - jnp.mean(output, axis=1, keepdims=True)
        inv_std = lax.rsqrt(jnp.mean(centred * centred, axis=1, keepdims=True) + norm_eps)
        normed = centred * inv_std
        scaled = grad_rows * gain_ref[...]
        norm_grad = inv_std * (
            scaled
            - jnp.mean(scaled, axis=1, keepdims=True)
            - normed * jnp.mean(scaled * normed, axis=1, keepdims=True)
        )
        norm_parts = split(norm_grad)
        hidden_grad = dot3(norm_parts, second, NT) * sigmoid_hidden * (1.0 + hidden * (1.0 - sigmoid_hidden))
        edge_out[at, :] = hidden_grad
        g_ref[part[0], :] += dot3(active, norm_parts, TN)
        small_ref[0:1, :] += jnp.sum(hidden_grad, axis=0, keepdims=True)
        small_ref[1:2, :] += jnp.sum(norm_grad, axis=0, keepdims=True)
        small_ref[2:3, :] += jnp.sum(grad_rows * normed, axis=0, keepdims=True)
        small_ref[3:4, :] += jnp.sum(grad_rows, axis=0, keepdims=True)

    loop(steps, step)

    def spread_sums(row, pieces, into):
        hidden_parts = split(edge_out[...])
        for k, piece in enumerate(pieces):
            line = k * node_rows + lax.broadcasted_iota(jnp.int32, (node_rows, slot_count), 0)
            into[piece] = dot2((row[...] == line).astype(jnp.float32).astype(jnp.bfloat16), hidden_parts)

    def outer(table, pieces, sums, rows):
        g_ref[rows, :] = jnp.zeros((width, width), jnp.float32)
        for piece in pieces:
            g_ref[rows, :] += dot3(split(table[piece]), split(sums[piece]), TN)

    used = 0
    scatters = []
    for axis, order, cols in plan["scatter"]:
        source, out = (ps_ref, own_s) if axis == "recv" else (pr_ref, own_r)
        scatters.append(
            scatter_stream(source, slots[used : used + len(order)], sems, base, axis, order, pl.ds(*cols), out, cols[1])
        )
        base += len(order)
        used += len(order)
    totals = []
    for order, cols, start in plan["total"]:
        totals.append(
            total_stream(
                g_ref, slots[used : used + len(order)], sems, base, order, start, 2 * width, pl.ds(*cols), g_out, factor
            )
        )
        base += 2 * len(order)
        used += len(order)
    early = [t for t, (_, _, start) in zip(totals, plan["total"]) if start == 0]
    late = [t for t, (_, _, start) in zip(totals, plan["total"]) if start != 0]

    spread_sums(rrow_ref, recv_pieces, pr_ref)
    for stream in scatters[1:]:
        next(stream)
    spread_sums(srow_ref, send_pieces, ps_ref)
    next(scatters[0])

    def edge_outer(i):
        at = rows_at(i)
        g_ref[part[1], :] += dot3(split(edge_ref[at, :]), split(edge_out[at, :]), TN)

    g_ref[part[1], :] = jnp.zeros((width, width), jnp.float32)
    loop(steps, edge_outer)
    small = small_stream(small_ref, small_slots, sems, base, plan["moves"], small_out, factor)
    for stream in early:
        next(stream)
    next(small)
    outer(ts_ref, send_pieces, ps_ref, part[2])
    outer(tr_ref, recv_pieces, pr_ref, part[3])
    for stream in late:
        next(stream)

    def finish():
        yield

        def edge_back(i):
            at = rows_at(i)
            edge_out[at, :] = cot_ref[at, :] + dot3(split(edge_out[at, :]), (wh[part[1], :], wl[part[1], :]), NT)

        loop(steps, edge_back)
        for _ in range(6):
            yield

    run_streams(scatters + early + late + [small, finish()])
    s_own[...] = dot3(split(own_s[...]), (wh[part[2], :], wl[part[2], :]), NT)
    r_own[...] = dot3(split(own_r[...]), (wh[part[3], :], wl[part[3], :]), NT)


def f32(*shape):
    return jax.ShapeDtypeStruct(shape, jnp.float32)


def make_plan(recv_bits, send_bits, width):
    half = width // 2
    recv_up = list(range(recv_bits))
    send_up = list(range(send_bits))
    recv_down, send_down = recv_up[::-1], send_up[::-1]
    recv_moves = [("recv", bit) for bit in recv_up]
    send_moves = [("send", bit) for bit in send_up]
    late_first = send_up[1:] + send_up[:1]
    return {
        "moves": recv_moves + send_moves,
        "gather": [
            ("recv", recv_down, (0, width)),
            ("send", send_down, (0, half)),
            ("send", send_up[:1] + send_down[:-1], (half, half)),
        ],
        "scatter": [
            ("recv", recv_up, (0, width)),
            ("send", send_up, (0, half)),
            ("send", late_first, (half, half)),
        ],
        "total": [
            (recv_moves + send_moves, (0, half), 0),
            (recv_moves[:1] + send_moves + recv_moves[1:], (half, half), 0),
            (recv_moves + send_moves, (0, half), 2 * width),
            (recv_moves[:1] + send_moves + recv_moves[1:], (half, half), 2 * width),
        ],
    }


def shards(
    latent,
    edge_feat,
    senders,
    receivers,
    live_blocks,
    cotangent,
    w_first,
    first_bias,
    w_second,
    second_bias,
    norm_gain,
):
    node_rows, width = latent.shape
    slot_count = edge_feat.shape[0]
    recv_count = lax.axis_size("recv")
    send_count = lax.axis_size("send")
    recv_bits, send_bits = bits_of(recv_count), bits_of(send_count)
    recv_index = lax.axis_index("recv")
    recv_local = receivers - recv_index * (send_count * node_rows)
    send_local = senders // node_rows // send_count * node_rows + senders % node_rows
    plan = make_plan(recv_bits, send_bits, width)
    factor = 1.0 / math.sqrt(slot_count * recv_count * send_count)
    vmem = pl.BlockSpec(memory_space=pltpu.VMEM)
    recv_shape = (2,) * recv_bits + (node_rows, width)
    send_shape = (2,) * send_bits + (node_rows, width)

    anywhere = pl.BlockSpec(memory_space=pl.ANY)
    smem = pl.BlockSpec(memory_space=pltpu.SMEM)
    half_type = jnp.bfloat16
    slots = []
    copies = sum(len(order) for _, order, _ in plan["gather"])
    for _, order, cols in plan["scatter"]:
        for at in range(len(order)):
            slots.append(pltpu.VMEM((2,) * (len(order) - 1 - at) + (node_rows, cols[1]), jnp.float32))
        copies += len(order)
    for order, cols, start in plan["total"]:
        for at in range(len(order)):
            slots.append(pltpu.VMEM((max(2 * width >> (at + 1), 8), cols[1]), jnp.float32))
        copies += 2 * len(order)
    moves = len(plan["moves"])
    copies += moves
    edge_out, send_grad, recv_grad, weights, small = pl.pallas_call(
        functools.partial(whole_kernel, plan, factor),
        out_shape=(
            f32(slot_count, width),
            f32(node_rows, width),
            f32(node_rows, width),
            f32(4 * width, width),
            f32(8, width),
        ),
        in_specs=[smem, vmem, anywhere, anywhere, vmem, vmem, vmem, vmem, anywhere, vmem, anywhere, vmem, vmem],
        out_specs=(vmem,) * 5,
        scratch_shapes=[
            pltpu.SemaphoreType.DMA((2, copies)),
            pltpu.SemaphoreType.DMA((4,)),
            pltpu.VMEM((slot_count, width), jnp.float32),
            pltpu.VMEM((slot_count, width), jnp.float32),
            pltpu.VMEM((4 * width, width), half_type),
            pltpu.VMEM((4 * width, width), half_type),
            pltpu.VMEM(recv_shape, jnp.float32),
            pltpu.VMEM(send_shape, jnp.float32),
            pltpu.VMEM(recv_shape, jnp.float32),
            pltpu.VMEM(send_shape, jnp.float32),
            pltpu.VMEM((4 * width, width), jnp.float32),
            pltpu.VMEM((8, width), jnp.float32),
            pltpu.VMEM((node_rows, width), jnp.float32),
            pltpu.VMEM((node_rows, width), jnp.float32),
            pltpu.VMEM((2 * moves, 8, width), jnp.float32),
        ]
        + slots,
        compiler_params=pltpu.CompilerParams(collective_id=0, has_side_effects=True, vmem_limit_bytes=60 << 20),
        name="edge_block",
    )(
        live_blocks,
        latent,
        edge_feat,
        cotangent,
        send_local[:, None],
        send_local[None, :],
        recv_local[:, None],
        recv_local[None, :],
        w_first,
        first_bias[None, :],
        w_second,
        second_bias[None, :],
        norm_gain[None, :],
    )
    return (edge_out, send_grad, recv_grad, weights[width:], weights[:width], small[:4])


def solution(mesh):
    return jax.shard_map(
        shards,
        mesh=mesh,
        in_specs=(
            P(("recv", "send"), None),
            P(("recv", "send"), None),
            P(("recv", "send")),
            P(("recv", "send")),
            P(("recv", "send")),
            P(("recv", "send"), None),
            P(),
            P(),
            P(),
            P(),
            P(),
        ),
        out_specs=(
            P(("recv", "send"), None),
            P(("recv", "send"), None),
            P(("recv", "send"), None),
            P(),
            P(),
            P(),
        ),
        check_vma=False,
    )
```

```python
import functools
import math

import jax
import jax.numpy as jnp
from jax import lax
from jax.experimental import pallas as pl
from jax.experimental.pallas import tpu as pltpu
from jax.sharding import PartitionSpec as P

norm_eps = 1e-05
block_rows = 128
step_rows = 256
MESH = pl.DeviceIdType.MESH
NN = (((1,), (0,)), ((), ()))
NT = (((1,), (1,)), ((), ()))
TN = (((0,), (0,)), ((), ()))


def split(value):
    high = value.astype(jnp.bfloat16)
    low = (value - high.astype(jnp.float32)).astype(jnp.bfloat16)
    return high, low


def mm(left, right, dims):
    return lax.dot_general(left, right, dims, preferred_element_type=jnp.float32)


def dot3(left, right, dims):
    return mm(left[0], right[0], dims) + mm(left[0], right[1], dims) + mm(left[1], right[0], dims)


def dot2(exact, right):
    return mm(exact, right[0], NN) + mm(exact, right[1], NN)


def bits_of(count):
    return max(count.bit_length() - 1, 0)


def my_bit(axis, bit):
    return (lax.axis_index(axis) // (1 << bit)) % 2


def partner_of(axis, bit):
    mine = my_bit(axis, bit)
    other = lax.axis_index(axis) + (1 - 2 * mine) * (1 << bit)
    if axis == "recv":
        return (other, lax.axis_index("send"))
    return (lax.axis_index("recv"), other)


def greet(moves):
    barrier = pltpu.get_barrier_semaphore()
    for axis, bit in moves:
        pl.semaphore_signal(barrier, inc=1, device_id=partner_of(axis, bit), device_id_type=MESH)
    pl.semaphore_wait(barrier, len(moves))


def run_streams(streams):
    live = list(streams)
    while live:
        after = []
        for stream in live:
            try:
                next(stream)
                after.append(stream)
            except StopIteration:
                pass
        live = after


def send_to(src, dst, sems, at, axis, bit):
    copy = pltpu.make_async_remote_copy(
        src_ref=src,
        dst_ref=dst,
        send_sem=sems.at[0, at],
        recv_sem=sems.at[1, at],
        device_id=partner_of(axis, bit),
        device_id_type=MESH,
    )
    copy.start()
    return copy


def gather_stream(table, sems, base, axis, order, cols):
    count = len(order)
    done = set()
    for at, bit in enumerate(order):
        index = []
        for dim in range(count):
            owner = count - 1 - dim
            index.append(pl.ds(0, 2) if owner in done else pl.ds(my_bit(axis, owner), 1))
        region = table.at[tuple(index) + (slice(None), cols)]
        copy = send_to(region, region, sems, base + at, axis, bit)
        yield
        copy.wait()
        done.add(bit)


def add_rows(dst, left, right, rows):
    chunk = min(rows, 64)

    def body(i, carry):
        at = pl.ds(pl.multiple_of(i * chunk, chunk), chunk)
        dst[at, :] = left[at, :] + right[at, :]
        return carry

    lax.fori_loop(0, rows // chunk, body, 0)


def scatter_stream(source, slots, sems, base, axis, order, cols, out, width):
    held = source
    left = sorted(order, reverse=True)
    for at, bit in enumerate(order):
        place = left.index(bit)
        mine = my_bit(axis, bit)
        pick = lambda ref, which: ref.at[(slice(None),) * place + (which,)]
        if at == 0:
            outgoing = source.at[(slice(None),) * place + (1 - mine,) + (slice(None),) * (len(left) - place) + (cols,)]
            kept = source.at[(slice(None),) * place + (mine,) + (slice(None),) * (len(left) - place) + (cols,)]
        else:
            outgoing, kept = pick(held, 1 - mine), pick(held, mine)
        slot = slots[at]
        copy = send_to(outgoing, slot, sems, base + at, axis, bit)
        yield
        copy.wait()
        left.remove(bit)
        lead = 1 << len(left)
        for piece in range(lead):
            at_piece = tuple((piece >> (len(left) - 1 - d)) & 1 for d in range(len(left)))
            target = out.at[:, cols] if not left else slot.at[at_piece]
            first = slot.at[at_piece] if left else slot
            second = kept.at[at_piece] if left else kept
            add_rows(target, first, second, block_rows)
        held = slot


def total_stream(source, slots, sems, base, order, start, rows, cols, out, factor):
    held, offset = source.at[pl.ds(start, rows), cols], 0
    trail = []
    for at, (axis, bit) in enumerate(order):
        slot = slots[at]
        if rows > 8:
            rows //= 2
            mine = my_bit(axis, bit)
            outgoing = held.at[pl.ds(pl.multiple_of((1 - mine) * rows, rows), rows)]
            kept = held.at[pl.ds(pl.multiple_of(mine * rows, rows), rows)]
            offset = offset + mine * rows
            trail.append((axis, bit, rows, offset))
        else:
            outgoing = kept = held
        copy = send_to(outgoing, slot, sems, base + at, axis, bit)
        yield
        copy.wait()
        add_rows(slot, slot, kept, rows)
        held = slot
    out[pl.ds(pl.multiple_of(start + offset, 8), rows), cols] = held[...] * factor
    base += len(order)
    for at, (axis, bit, rows, offset) in enumerate(reversed(trail)):
        region = out.at[pl.ds(pl.multiple_of(start + offset, 8), rows), cols]
        copy = send_to(region, region, sems, base + at, axis, bit)
        yield
        copy.wait()


def small_stream(source, slots, sems, base, order, out, factor):
    for at, (axis, bit) in enumerate(order):
        held = source if at == 0 else slots.at[2 * at - 1]
        copy = send_to(held, slots.at[2 * at], sems, base + at, axis, bit)
        yield
        copy.wait()
        slots[2 * at + 1] = held[...] + slots[2 * at]
    out[...] = slots[2 * len(order) - 1, : out.shape[0], :] * factor


def rows_at(i, rows=step_rows):
    return pl.ds(pl.multiple_of(i * rows, rows), rows)


def loop(count, body):
    def run(i, carry):
        body(i)
        return carry

    lax.fori_loop(0, count, run, 0)


def whole_kernel(
    plan,
    factor,
    live_ref,
    latent_ref,
    edge_hbm,
    cot_hbm,
    srow_ref,
    rrow_ref,
    w1_hbm,
    b1_ref,
    w2_hbm,
    b2_ref,
    gain_ref,
    edge_hbm_out,
    s_own,
    r_own,
    w1_hbm_out,
    w2_hbm_out,
    small_out,
    sems,
    local_sems,
    edge_out,
    g_out,
    scol_ref,
    rcol_ref,
    edge_ref,
    cot_ref,
    wh,
    wl,
    ts_ref,
    tr_ref,
    ps_ref,
    pr_ref,
    g_ref,
    small_ref,
    own_s,
    own_r,
    small_slots,
    *slots,
):
    slot_count, width = edge_ref.shape
    steps = slot_count // step_rows
    live_limit = block_rows * live_ref[0]
    part = [pl.ds(k * width, width) for k in range(4)]
    node_rows = latent_ref.shape[0]
    send_pieces = [tuple((k >> (ts_ref.ndim - 3 - d)) & 1 for d in range(ts_ref.ndim - 2)) for k in range(1 << (ts_ref.ndim - 2))]
    recv_pieces = [tuple((k >> (tr_ref.ndim - 3 - d)) & 1 for d in range(tr_ref.ndim - 2)) for k in range(1 << (tr_ref.ndim - 2))]

    loads = [
        pltpu.make_async_copy(w2_hbm, g_out.at[part[0]], local_sems.at[0]),
        pltpu.make_async_copy(w1_hbm, g_out.at[pl.ds(width, 3 * width)], local_sems.at[1]),
        pltpu.make_async_copy(edge_hbm, edge_ref, local_sems.at[2]),
        pltpu.make_async_copy(cot_hbm, cot_ref, local_sems.at[3]),
    ]
    for load in loads:
        load.start()
    for table, axis in ((ts_ref, "recv"), (tr_ref, "send")):
        count = table.ndim - 2
        at = tuple(my_bit(axis, count - 1 - dim) for dim in range(count))
        table[at] = latent_ref[...]
    greet(plan["moves"])

    streams = []
    base = 0
    for axis, order, cols in plan["gather"]:
        table = ts_ref if axis == "recv" else tr_ref
        streams.append(gather_stream(table, sems, base, axis, order, pl.ds(*cols)))
        base += len(order)

    send_stride = lax.axis_size("send") * node_rows
    send_first = lax.axis_index("send") * node_rows
    recv_first = lax.axis_index("recv") * send_stride
    node_shift = node_rows.bit_length() - 1

    def prepare():
        for k in range(slot_count // 128):
            at = pl.ds(k * 128, 128)
            scol_ref[at, :] = jnp.broadcast_to(srow_ref[:, at], (128, 128)).T - send_first
            rcol_ref[at, :] = jnp.broadcast_to(rrow_ref[:, at], (128, 128)).T - recv_first
        yield
        for load in loads:
            load.wait()

        def split_rows(i):
            at = rows_at(i)
            wh[at, :], wl[at, :] = split(g_out[at, :])

        loop(4 * width // step_rows, split_rows)

        def first_part(i):
            at = rows_at(i)
            edge_out[at, :] = dot3(split(edge_ref[at, :]), (wh[part[1], :], wl[part[1], :]), NN) + b1_ref[...]

        loop(steps, first_part)
        yield
        project(ts_ref, send_pieces, ps_ref, part[2])

    def project(table, pieces, into, rows):
        for k, piece in enumerate(pieces):
            into[piece] = dot3(split(table[piece]), (wh[rows, :], wl[rows, :]), NN)

    run_streams(streams + [prepare()])
    project(tr_ref, recv_pieces, pr_ref, part[3])

    small_ref[...] = jnp.zeros_like(small_ref)
    g_ref[part[0], :] = jnp.zeros((width, width), jnp.float32)
    send_nodes, recv_nodes = len(send_pieces) * node_rows, len(recv_pieces) * node_rows

    def step(i):
        at = rows_at(i)
        position = i * step_rows + lax.broadcasted_iota(jnp.int32, (step_rows, 1), 0)
        grad_rows = cot_ref[at, :] * (position < live_limit).astype(jnp.float32)
        cot_ref[at, :] = grad_rows

        def pick(col, nodes, gap):
            lane = lax.broadcasted_iota(jnp.int32, (1, nodes), 1)
            lane = lane + lax.shift_right_arithmetic(lane, jnp.int32(node_shift)) * gap
            return (col[at, 0:1] == lane).astype(jnp.float32).astype(jnp.bfloat16)

        send_table = split(ps_ref[...].reshape(send_nodes, width))
        recv_table = split(pr_ref[...].reshape(recv_nodes, width))
        hidden = edge_out[at, :] + dot2(pick(scol_ref, send_nodes, send_stride - node_rows), send_table)
        hidden = hidden + dot2(pick(rcol_ref, recv_nodes, 0), recv_table)
        sigmoid_hidden = jax.nn.sigmoid(hidden)
        active = split(hidden * sigmoid_hidden)
        second = (wh[part[0], :], wl[part[0], :])
        output = dot3(active, second, NN) + b2_ref[...]
        centred = output - jnp.mean(output, axis=1, keepdims=True)
        inv_std = lax.rsqrt(jnp.mean(centred * centred, axis=1, keepdims=True) + norm_eps)
        normed = centred * inv_std
        scaled = grad_rows * gain_ref[...]
        norm_grad = inv_std * (
            scaled
            - jnp.mean(scaled, axis=1, keepdims=True)
            - normed * jnp.mean(scaled * normed, axis=1, keepdims=True)
        )
        norm_parts = split(norm_grad)
        hidden_grad = dot3(norm_parts, second, NT) * sigmoid_hidden * (1.0 + hidden * (1.0 - sigmoid_hidden))
        edge_out[at, :] = hidden_grad
        g_ref[part[0], :] += dot3(active, norm_parts, TN)
        small_ref[0:1, :] += jnp.sum(hidden_grad, axis=0, keepdims=True)
        small_ref[1:2, :] += jnp.sum(norm_grad, axis=0, keepdims=True)
        small_ref[2:3, :] += jnp.sum(grad_rows * normed, axis=0, keepdims=True)
        small_ref[3:4, :] += jnp.sum(grad_rows, axis=0, keepdims=True)

    loop(steps, step)

    def spread_sums(row, pieces, into, first, stride):
        hidden_parts = split(edge_out[...])
        for k, piece in enumerate(pieces):
            line = first + k * stride + lax.broadcasted_iota(jnp.int32, (node_rows, slot_count), 0)
            into[piece] = dot2((row[...] == line).astype(jnp.float32).astype(jnp.bfloat16), hidden_parts)

    def outer(table, pieces, sums, rows):
        g_ref[rows, :] = jnp.zeros((width, width), jnp.float32)
        for piece in pieces:
            g_ref[rows, :] += dot3(split(table[piece]), split(sums[piece]), TN)

    used = 0
    scatters = []
    for axis, order, cols in plan["scatter"]:
        source, out = (ps_ref, own_s) if axis == "recv" else (pr_ref, own_r)
        scatters.append(
            scatter_stream(source, slots[used : used + len(order)], sems, base, axis, order, pl.ds(*cols), out, cols[1])
        )
        base += len(order)
        used += len(order)
    totals = []
    for order, cols, start in plan["total"]:
        totals.append(
            total_stream(
                g_ref, slots[used : used + len(order)], sems, base, order, start, 2 * width, pl.ds(*cols), g_out, factor
            )
        )
        base += 2 * len(order)
        used += len(order)
    early = [t for t, (_, _, start) in zip(totals, plan["total"]) if start == 0]
    late = [t for t, (_, _, start) in zip(totals, plan["total"]) if start != 0]

    spread_sums(rrow_ref, recv_pieces, pr_ref, recv_first, node_rows)
    for stream in scatters[1:]:
        next(stream)
    spread_sums(srow_ref, send_pieces, ps_ref, send_first, send_stride)
    next(scatters[0])

    def edge_outer(i):
        at = rows_at(i)
        g_ref[part[1], :] += dot3(split(edge_ref[at, :]), split(edge_out[at, :]), TN)

    g_ref[part[1], :] = jnp.zeros((width, width), jnp.float32)
    loop(steps, edge_outer)
    small = small_stream(small_ref, small_slots, sems, base, plan["moves"], small_out, factor)
    for stream in early:
        next(stream)
    next(small)
    outer(ts_ref, send_pieces, ps_ref, part[2])
    outer(tr_ref, recv_pieces, pr_ref, part[3])
    for stream in late:
        next(stream)

    edge_store = pltpu.make_async_copy(edge_out, edge_hbm_out, local_sems.at[2])

    def finish():
        def edge_back(i):
            at = rows_at(i)
            edge_out[at, :] = cot_ref[at, :] + dot3(split(edge_out[at, :]), (wh[part[1], :], wl[part[1], :]), NT)

        loop(steps, edge_back)
        edge_store.start()
        yield

    run_streams(early + late + [small, finish()] + scatters)
    stores = [
        pltpu.make_async_copy(g_out.at[part[0]], w2_hbm_out, local_sems.at[0]),
        pltpu.make_async_copy(g_out.at[pl.ds(width, 3 * width)], w1_hbm_out, local_sems.at[1]),
    ]
    for store in stores:
        store.start()
    s_own[...] = dot3(split(own_s[...]), (wh[part[2], :], wl[part[2], :]), NT)
    r_own[...] = dot3(split(own_r[...]), (wh[part[3], :], wl[part[3], :]), NT)
    for store in stores + [edge_store]:
        store.wait()


def f32(*shape):
    return jax.ShapeDtypeStruct(shape, jnp.float32)


def make_plan(recv_bits, send_bits, width):
    half = width // 2
    most = width // 4 * 3
    recv_up = list(range(recv_bits))
    send_up = list(range(send_bits))
    recv_down, send_down = recv_up[::-1], send_up[::-1]
    recv_moves = [("recv", bit) for bit in recv_up]
    send_moves = [("send", bit) for bit in send_up]
    late_first = send_up[1:] + send_up[:1]
    return {
        "moves": recv_moves + send_moves,
        "gather": [
            ("recv", recv_down, (0, width)),
            ("send", send_down, (0, most)),
            ("send", send_up[:1] + send_down[:-1], (most, width - most)),
        ],
        "scatter": [
            ("recv", recv_up, (0, width)),
            ("send", send_up, (0, most)),
            ("send", late_first, (most, width - most)),
        ],
        "total": [
            (recv_moves + send_moves, (0, half), 0),
            (recv_moves + send_moves, (half, half), 0),
            (recv_moves + send_moves, (0, half), 2 * width),
            (recv_moves[:1] + send_moves + recv_moves[1:], (half, half), 2 * width),
        ],
    }


def shards(
    latent,
    edge_feat,
    senders,
    receivers,
    live_blocks,
    cotangent,
    w_first,
    first_bias,
    w_second,
    second_bias,
    norm_gain,
):
    node_rows, width = latent.shape
    slot_count = edge_feat.shape[0]
    recv_count = lax.axis_size("recv")
    send_count = lax.axis_size("send")
    recv_bits, send_bits = bits_of(recv_count), bits_of(send_count)
    plan = make_plan(recv_bits, send_bits, width)
    factor = 1.0 / math.sqrt(slot_count * recv_count * send_count)
    vmem = pl.BlockSpec(memory_space=pltpu.VMEM)
    recv_shape = (2,) * recv_bits + (node_rows, width)
    send_shape = (2,) * send_bits + (node_rows, width)

    anywhere = pl.BlockSpec(memory_space=pl.ANY)
    smem = pl.BlockSpec(memory_space=pltpu.SMEM)
    half_type = jnp.bfloat16
    slots = []
    copies = sum(len(order) for _, order, _ in plan["gather"])
    for _, order, cols in plan["scatter"]:
        for at in range(len(order)):
            slots.append(pltpu.VMEM((2,) * (len(order) - 1 - at) + (node_rows, cols[1]), jnp.float32))
        copies += len(order)
    for order, cols, start in plan["total"]:
        for at in range(len(order)):
            slots.append(pltpu.VMEM((max(2 * width >> (at + 1), 8), cols[1]), jnp.float32))
        copies += 2 * len(order)
    moves = len(plan["moves"])
    copies += moves
    return pl.pallas_call(
        functools.partial(whole_kernel, plan, factor),
        out_shape=(
            f32(slot_count, width),
            f32(node_rows, width),
            f32(node_rows, width),
            f32(3 * width, width),
            f32(width, width),
            f32(4, width),
        ),
        in_specs=[smem, vmem, anywhere, anywhere, vmem, vmem, anywhere, vmem, anywhere, vmem, vmem],
        out_specs=(anywhere, vmem, vmem, anywhere, anywhere, vmem),
        scratch_shapes=[
            pltpu.SemaphoreType.DMA((2, copies)),
            pltpu.SemaphoreType.DMA((4,)),
            pltpu.VMEM((slot_count, width), jnp.float32),
            pltpu.VMEM((4 * width, width), jnp.float32),
            pltpu.VMEM((slot_count, 128), jnp.int32),
            pltpu.VMEM((slot_count, 128), jnp.int32),
            pltpu.VMEM((slot_count, width), jnp.float32),
            pltpu.VMEM((slot_count, width), jnp.float32),
            pltpu.VMEM((4 * width, width), half_type),
            pltpu.VMEM((4 * width, width), half_type),
            pltpu.VMEM(recv_shape, jnp.float32),
            pltpu.VMEM(send_shape, jnp.float32),
            pltpu.VMEM(recv_shape, jnp.float32),
            pltpu.VMEM(send_shape, jnp.float32),
            pltpu.VMEM((4 * width, width), jnp.float32),
            pltpu.VMEM((8, width), jnp.float32),
            pltpu.VMEM((node_rows, width), jnp.float32),
            pltpu.VMEM((node_rows, width), jnp.float32),
            pltpu.VMEM((2 * moves, 8, width), jnp.float32),
        ]
        + slots,
        compiler_params=pltpu.CompilerParams(collective_id=0, has_side_effects=True, vmem_limit_bytes=60 << 20),
        name="edge_block",
    )(
        live_blocks,
        latent,
        edge_feat,
        cotangent,
        senders[None, :],
        receivers[None, :],
        w_first,
        first_bias[None, :],
        w_second,
        second_bias[None, :],
        norm_gain[None, :],
    )


def solution(mesh):
    return jax.shard_map(
        shards,
        mesh=mesh,
        in_specs=(
            P(("recv", "send"), None),
            P(("recv", "send"), None),
            P(("recv", "send")),
            P(("recv", "send")),
            P(("recv", "send")),
            P(("recv", "send"), None),
            P(),
            P(),
            P(),
            P(),
            P(),
        ),
        out_specs=(
            P(("recv", "send"), None),
            P(("recv", "send"), None),
            P(("recv", "send"), None),
            P(),
            P(),
            P(),
        ),
        check_vma=False,
    )
```

```python
import functools
import math

import jax
import jax.numpy as jnp
from jax import lax
from jax.experimental import pallas as pl
from jax.experimental.pallas import tpu as pltpu
from jax.sharding import PartitionSpec as P

norm_eps = 1e-05
block_rows = 128
step_rows = 256
MESH = pl.DeviceIdType.MESH
NN = (((1,), (0,)), ((), ()))
NT = (((1,), (1,)), ((), ()))
TN = (((0,), (0,)), ((), ()))


def split(value):
    high = value.astype(jnp.bfloat16)
    low = (value - high.astype(jnp.float32)).astype(jnp.bfloat16)
    return high, low


def mm(left, right, dims):
    return lax.dot_general(left, right, dims, preferred_element_type=jnp.float32)


def dot3(left, right, dims):
    return mm(left[0], right[0], dims) + mm(left[0], right[1], dims) + mm(left[1], right[0], dims)


def dot2(exact, right):
    return mm(exact, right[0], NN) + mm(exact, right[1], NN)


def bits_of(count):
    return max(count.bit_length() - 1, 0)


def my_bit(axis, bit):
    return (lax.axis_index(axis) // (1 << bit)) % 2


def partner_of(axis, bit):
    mine = my_bit(axis, bit)
    other = lax.axis_index(axis) + (1 - 2 * mine) * (1 << bit)
    if axis == "recv":
        return (other, lax.axis_index("send"))
    return (lax.axis_index("recv"), other)


def greet(moves):
    barrier = pltpu.get_barrier_semaphore()
    for axis, bit in moves:
        pl.semaphore_signal(barrier, inc=1, device_id=partner_of(axis, bit), device_id_type=MESH)
    pl.semaphore_wait(barrier, len(moves))


def run_streams(streams):
    live = list(streams)
    while live:
        after = []
        for stream in live:
            try:
                next(stream)
                after.append(stream)
            except StopIteration:
                pass
        live = after


def send_to(src, dst, sems, at, axis, bit):
    copy = pltpu.make_async_remote_copy(
        src_ref=src,
        dst_ref=dst,
        send_sem=sems.at[0, at],
        recv_sem=sems.at[1, at],
        device_id=partner_of(axis, bit),
        device_id_type=MESH,
    )
    copy.start()
    return copy


def gather_stream(table, sems, base, axis, order, cols):
    count = len(order)
    done = set()
    for at, bit in enumerate(order):
        index = []
        for dim in range(count):
            owner = count - 1 - dim
            index.append(pl.ds(0, 2) if owner in done else pl.ds(my_bit(axis, owner), 1))
        region = table.at[tuple(index) + (slice(None), cols)]
        copy = send_to(region, region, sems, base + at, axis, bit)
        yield
        copy.wait()
        done.add(bit)


def add_rows(dst, left, right, rows):
    chunk = min(rows, 64)

    def body(i, carry):
        at = pl.ds(pl.multiple_of(i * chunk, chunk), chunk)
        dst[at, :] = left[at, :] + right[at, :]
        return carry

    lax.fori_loop(0, rows // chunk, body, 0)


def scatter_stream(source, slots, sems, base, axis, order, cols, out, width):
    held = source
    left = sorted(order, reverse=True)
    for at, bit in enumerate(order):
        place = left.index(bit)
        mine = my_bit(axis, bit)
        pick = lambda ref, which: ref.at[(slice(None),) * place + (which,)]
        if at == 0:
            outgoing = source.at[(slice(None),) * place + (1 - mine,) + (slice(None),) * (len(left) - place) + (cols,)]
            kept = source.at[(slice(None),) * place + (mine,) + (slice(None),) * (len(left) - place) + (cols,)]
        else:
            outgoing, kept = pick(held, 1 - mine), pick(held, mine)
        slot = slots[at]
        copy = send_to(outgoing, slot, sems, base + at, axis, bit)
        yield
        copy.wait()
        left.remove(bit)
        lead = 1 << len(left)
        for piece in range(lead):
            at_piece = tuple((piece >> (len(left) - 1 - d)) & 1 for d in range(len(left)))
            target = out.at[:, cols] if not left else slot.at[at_piece]
            first = slot.at[at_piece] if left else slot
            second = kept.at[at_piece] if left else kept
            add_rows(target, first, second, block_rows)
        held = slot


def total_stream(source, slots, sems, base, order, start, rows, cols, out, factor):
    held, offset = source.at[pl.ds(start, rows), cols], 0
    trail = []
    for at, (axis, bit) in enumerate(order):
        slot = slots[at]
        if rows > 8:
            rows //= 2
            mine = my_bit(axis, bit)
            outgoing = held.at[pl.ds(pl.multiple_of((1 - mine) * rows, rows), rows)]
            kept = held.at[pl.ds(pl.multiple_of(mine * rows, rows), rows)]
            offset = offset + mine * rows
            trail.append((axis, bit, rows, offset))
        else:
            outgoing = kept = held
        copy = send_to(outgoing, slot, sems, base + at, axis, bit)
        yield
        copy.wait()
        add_rows(slot, slot, kept, rows)
        held = slot
    out[pl.ds(pl.multiple_of(start + offset, 8), rows), cols] = held[...] * factor
    base += len(order)
    for at, (axis, bit, rows, offset) in enumerate(reversed(trail)):
        region = out.at[pl.ds(pl.multiple_of(start + offset, 8), rows), cols]
        copy = send_to(region, region, sems, base + at, axis, bit)
        yield
        copy.wait()


def small_stream(source, slots, sems, base, order, out, factor):
    for at, (axis, bit) in enumerate(order):
        held = source if at == 0 else slots.at[2 * at - 1]
        copy = send_to(held, slots.at[2 * at], sems, base + at, axis, bit)
        yield
        copy.wait()
        slots[2 * at + 1] = held[...] + slots[2 * at]
    out[...] = slots[2 * len(order) - 1, : out.shape[0], :] * factor


def rows_at(i, rows=step_rows):
    return pl.ds(pl.multiple_of(i * rows, rows), rows)


def loop(count, body):
    def run(i, carry):
        body(i)
        return carry

    lax.fori_loop(0, count, run, 0)


def whole_kernel(
    plan,
    factor,
    live_ref,
    latent_ref,
    edge_hbm,
    cot_hbm,
    srow_ref,
    rrow_ref,
    w1_hbm,
    b1_ref,
    w2_hbm,
    b2_ref,
    gain_ref,
    edge_hbm_out,
    s_own,
    r_own,
    w1_hbm_out,
    w2_hbm_out,
    small_out,
    sems,
    local_sems,
    edge_out,
    g_out,
    scol_ref,
    rcol_ref,
    edge_ref,
    cot_ref,
    wh,
    wl,
    ts_ref,
    tr_ref,
    ps_ref,
    pr_ref,
    g_ref,
    small_ref,
    own_s,
    own_r,
    small_slots,
    *slots,
):
    slot_count, width = edge_ref.shape
    steps = slot_count // step_rows
    live_limit = block_rows * live_ref[0]
    part = [pl.ds(k * width, width) for k in range(4)]
    node_rows = latent_ref.shape[0]
    send_pieces = [tuple((k >> (ts_ref.ndim - 3 - d)) & 1 for d in range(ts_ref.ndim - 2)) for k in range(1 << (ts_ref.ndim - 2))]
    recv_pieces = [tuple((k >> (tr_ref.ndim - 3 - d)) & 1 for d in range(tr_ref.ndim - 2)) for k in range(1 << (tr_ref.ndim - 2))]

    loads = [
        pltpu.make_async_copy(w2_hbm, g_out.at[part[0]], local_sems.at[0]),
        pltpu.make_async_copy(w1_hbm, g_out.at[pl.ds(width, 3 * width)], local_sems.at[1]),
        pltpu.make_async_copy(edge_hbm, edge_ref, local_sems.at[2]),
        pltpu.make_async_copy(cot_hbm, cot_ref, local_sems.at[3]),
    ]
    for load in loads:
        load.start()
    for table, axis in ((ts_ref, "recv"), (tr_ref, "send")):
        count = table.ndim - 2
        at = tuple(my_bit(axis, count - 1 - dim) for dim in range(count))
        table[at] = latent_ref[...]
    greet(plan["moves"])

    streams = []
    base = 0
    for axis, order, cols in plan["gather"]:
        table = ts_ref if axis == "recv" else tr_ref
        streams.append(gather_stream(table, sems, base, axis, order, pl.ds(*cols)))
        base += len(order)

    send_stride = lax.axis_size("send") * node_rows
    send_first = lax.axis_index("send") * node_rows
    recv_first = lax.axis_index("recv") * send_stride
    node_shift = node_rows.bit_length() - 1

    def prepare():
        for k in range(slot_count // 128):
            at = pl.ds(k * 128, 128)
            scol_ref[at, :] = jnp.broadcast_to(srow_ref[:, at], (128, 128)).T - send_first
            rcol_ref[at, :] = jnp.broadcast_to(rrow_ref[:, at], (128, 128)).T - recv_first
        yield
        for load in loads:
            load.wait()

        def split_rows(i):
            at = rows_at(i)
            wh[at, :], wl[at, :] = split(g_out[at, :])

        loop(4 * width // step_rows, split_rows)

        def first_part(i):
            at = rows_at(i)
            edge_out[at, :] = dot3(split(edge_ref[at, :]), (wh[part[1], :], wl[part[1], :]), NN) + b1_ref[...]

        loop(steps, first_part)
        yield
        project(ts_ref, send_pieces, ps_ref, part[2])

    def project(table, pieces, into, rows):
        for k, piece in enumerate(pieces):
            into[piece] = dot3(split(table[piece]), (wh[rows, :], wl[rows, :]), NN)

    run_streams(streams + [prepare()])
    project(tr_ref, recv_pieces, pr_ref, part[3])

    small_ref[...] = jnp.zeros_like(small_ref)
    g_ref[part[0], :] = jnp.zeros((width, width), jnp.float32)
    send_nodes, recv_nodes = len(send_pieces) * node_rows, len(recv_pieces) * node_rows

    def step(i):
        at = rows_at(i)
        position = i * step_rows + lax.broadcasted_iota(jnp.int32, (step_rows, 1), 0)
        grad_rows = cot_ref[at, :] * (position < live_limit).astype(jnp.float32)
        cot_ref[at, :] = grad_rows

        def pick(col, nodes, gap):
            lane = lax.broadcasted_iota(jnp.int32, (1, nodes), 1)
            lane = lane + lax.shift_right_arithmetic(lane, jnp.int32(node_shift)) * gap
            return (col[at, 0:1] == lane).astype(jnp.float32).astype(jnp.bfloat16)

        send_table = split(ps_ref[...].reshape(send_nodes, width))
        recv_table = split(pr_ref[...].reshape(recv_nodes, width))
        hidden = edge_out[at, :] + dot2(pick(scol_ref, send_nodes, send_stride - node_rows), send_table)
        hidden = hidden + dot2(pick(rcol_ref, recv_nodes, 0), recv_table)
        sigmoid_hidden = jax.nn.sigmoid(hidden)
        active = split(hidden * sigmoid_hidden)
        second = (wh[part[0], :], wl[part[0], :])
        output = dot3(active, second, NN) + b2_ref[...]
        centred = output - jnp.mean(output, axis=1, keepdims=True)
        inv_std = lax.rsqrt(jnp.mean(centred * centred, axis=1, keepdims=True) + norm_eps)
        normed = centred * inv_std
        scaled = grad_rows * gain_ref[...]
        norm_grad = inv_std * (
            scaled
            - jnp.mean(scaled, axis=1, keepdims=True)
            - normed * jnp.mean(scaled * normed, axis=1, keepdims=True)
        )
        norm_parts = split(norm_grad)
        hidden_grad = dot3(norm_parts, second, NT) * sigmoid_hidden * (1.0 + hidden * (1.0 - sigmoid_hidden))
        edge_out[at, :] = hidden_grad
        g_ref[part[0], :] += dot3(active, norm_parts, TN)
        small_ref[0:1, :] += jnp.sum(hidden_grad, axis=0, keepdims=True)
        small_ref[1:2, :] += jnp.sum(norm_grad, axis=0, keepdims=True)
        small_ref[2:3, :] += jnp.sum(grad_rows * normed, axis=0, keepdims=True)
        small_ref[3:4, :] += jnp.sum(grad_rows, axis=0, keepdims=True)

    loop(steps, step)

    def spread_sums(row, pieces, into, first, stride):
        hidden_parts = split(edge_out[...])
        for k, piece in enumerate(pieces):
            line = first + k * stride + lax.broadcasted_iota(jnp.int32, (node_rows, slot_count), 0)
            into[piece] = dot2((row[...] == line).astype(jnp.float32).astype(jnp.bfloat16), hidden_parts)

    def outer(table, pieces, sums, rows):
        g_ref[rows, :] = jnp.zeros((width, width), jnp.float32)
        for piece in pieces:
            g_ref[rows, :] += dot3(split(table[piece]), split(sums[piece]), TN)

    used = 0
    scatters = []
    for axis, order, cols in plan["scatter"]:
        source, out = (ps_ref, own_s) if axis == "recv" else (pr_ref, own_r)
        scatters.append(
            scatter_stream(source, slots[used : used + len(order)], sems, base, axis, order, pl.ds(*cols), out, cols[1])
        )
        base += len(order)
        used += len(order)
    totals = []
    for order, cols, start in plan["total"]:
        totals.append(
            total_stream(
                g_ref, slots[used : used + len(order)], sems, base, order, start, 2 * width, pl.ds(*cols), g_out, factor
            )
        )
        base += 2 * len(order)
        used += len(order)
    early = [t for t, (_, _, start) in zip(totals, plan["total"]) if start == 0]
    late = [t for t, (_, _, start) in zip(totals, plan["total"]) if start != 0]

    spread_sums(rrow_ref, recv_pieces, pr_ref, recv_first, node_rows)
    for stream in scatters[1:]:
        next(stream)
    spread_sums(srow_ref, send_pieces, ps_ref, send_first, send_stride)
    next(scatters[0])

    def edge_outer(i):
        at = rows_at(i)
        g_ref[part[1], :] += dot3(split(edge_ref[at, :]), split(edge_out[at, :]), TN)

    g_ref[part[1], :] = jnp.zeros((width, width), jnp.float32)
    loop(steps, edge_outer)
    small = small_stream(small_ref, small_slots, sems, base, plan["moves"], small_out, factor)
    for stream in early:
        next(stream)
    next(small)
    outer(ts_ref, send_pieces, ps_ref, part[2])
    outer(tr_ref, recv_pieces, pr_ref, part[3])
    for stream in late:
        next(stream)

    edge_store = pltpu.make_async_copy(edge_out, edge_hbm_out, local_sems.at[2])

    def finish():
        yield

        def edge_back(i):
            at = rows_at(i)
            edge_out[at, :] = cot_ref[at, :] + dot3(split(edge_out[at, :]), (wh[part[1], :], wl[part[1], :]), NT)

        loop(steps, edge_back)
        edge_store.start()
        yield

    run_streams(scatters + early + late + [small, finish()])
    stores = [
        pltpu.make_async_copy(g_out.at[part[0]], w2_hbm_out, local_sems.at[0]),
        pltpu.make_async_copy(g_out.at[pl.ds(width, 3 * width)], w1_hbm_out, local_sems.at[1]),
    ]
    for store in stores:
        store.start()
    s_own[...] = dot3(split(own_s[...]), (wh[part[2], :], wl[part[2], :]), NT)
    r_own[...] = dot3(split(own_r[...]), (wh[part[3], :], wl[part[3], :]), NT)
    for store in stores + [edge_store]:
        store.wait()


def f32(*shape):
    return jax.ShapeDtypeStruct(shape, jnp.float32)


def make_plan(recv_bits, send_bits, width):
    half = width // 2
    most = width // 2
    recv_up = list(range(recv_bits))
    send_up = list(range(send_bits))
    recv_down, send_down = recv_up[::-1], send_up[::-1]
    recv_moves = [("recv", bit) for bit in recv_up]
    send_moves = [("send", bit) for bit in send_up]
    late_first = send_up[1:] + send_up[:1]
    return {
        "moves": recv_moves + send_moves,
        "gather": [
            ("recv", recv_down, (0, width)),
            ("send", send_down, (0, most)),
            ("send", send_up[:1] + send_down[:-1], (most, width - most)),
        ],
        "scatter": [
            ("recv", recv_up, (0, width)),
            ("send", send_up, (0, most)),
            ("send", late_first, (most, width - most)),
        ],
        "total": [
            (recv_moves + send_moves, (0, half), 0),
            (recv_moves[:1] + send_moves + recv_moves[1:], (half, half), 0),
            (recv_moves + send_moves, (0, half), 2 * width),
            (recv_moves[:1] + send_moves + recv_moves[1:], (half, half), 2 * width),
        ],
    }


def shards(
    latent,
    edge_feat,
    senders,
    receivers,
    live_blocks,
    cotangent,
    w_first,
    first_bias,
    w_second,
    second_bias,
    norm_gain,
):
    node_rows, width = latent.shape
    slot_count = edge_feat.shape[0]
    recv_count = lax.axis_size("recv")
    send_count = lax.axis_size("send")
    recv_bits, send_bits = bits_of(recv_count), bits_of(send_count)
    plan = make_plan(recv_bits, send_bits, width)
    factor = 1.0 / math.sqrt(slot_count * recv_count * send_count)
    vmem = pl.BlockSpec(memory_space=pltpu.VMEM)
    recv_shape = (2,) * recv_bits + (node_rows, width)
    send_shape = (2,) * send_bits + (node_rows, width)

    anywhere = pl.BlockSpec(memory_space=pl.ANY)
    smem = pl.BlockSpec(memory_space=pltpu.SMEM)
    half_type = jnp.bfloat16
    slots = []
    copies = sum(len(order) for _, order, _ in plan["gather"])
    for _, order, cols in plan["scatter"]:
        for at in range(len(order)):
            slots.append(pltpu.VMEM((2,) * (len(order) - 1 - at) + (node_rows, cols[1]), jnp.float32))
        copies += len(order)
    for order, cols, start in plan["total"]:
        for at in range(len(order)):
            slots.append(pltpu.VMEM((max(2 * width >> (at + 1), 8), cols[1]), jnp.float32))
        copies += 2 * len(order)
    moves = len(plan["moves"])
    copies += moves
    return pl.pallas_call(
        functools.partial(whole_kernel, plan, factor),
        out_shape=(
            f32(slot_count, width),
            f32(node_rows, width),
            f32(node_rows, width),
            f32(3 * width, width),
            f32(width, width),
            f32(4, width),
        ),
        in_specs=[smem, vmem, anywhere, anywhere, vmem, vmem, anywhere, vmem, anywhere, vmem, vmem],
        out_specs=(anywhere, vmem, vmem, anywhere, anywhere, vmem),
        scratch_shapes=[
            pltpu.SemaphoreType.DMA((2, copies)),
            pltpu.SemaphoreType.DMA((4,)),
            pltpu.VMEM((slot_count, width), jnp.float32),
            pltpu.VMEM((4 * width, width), jnp.float32),
            pltpu.VMEM((slot_count, 128), jnp.int32),
            pltpu.VMEM((slot_count, 128), jnp.int32),
            pltpu.VMEM((slot_count, width), jnp.float32),
            pltpu.VMEM((slot_count, width), jnp.float32),
            pltpu.VMEM((4 * width, width), half_type),
            pltpu.VMEM((4 * width, width), half_type),
            pltpu.VMEM(recv_shape, jnp.float32),
            pltpu.VMEM(send_shape, jnp.float32),
            pltpu.VMEM(recv_shape, jnp.float32),
            pltpu.VMEM(send_shape, jnp.float32),
            pltpu.VMEM((4 * width, width), jnp.float32),
            pltpu.VMEM((8, width), jnp.float32),
            pltpu.VMEM((node_rows, width), jnp.float32),
            pltpu.VMEM((node_rows, width), jnp.float32),
            pltpu.VMEM((2 * moves, 8, width), jnp.float32),
        ]
        + slots,
        compiler_params=pltpu.CompilerParams(collective_id=0, has_side_effects=True, vmem_limit_bytes=60 << 20),
        name="edge_block",
    )(
        live_blocks,
        latent,
        edge_feat,
        cotangent,
        senders[None, :],
        receivers[None, :],
        w_first,
        first_bias[None, :],
        w_second,
        second_bias[None, :],
        norm_gain[None, :],
    )


def solution(mesh):
    return jax.shard_map(
        shards,
        mesh=mesh,
        in_specs=(
            P(("recv", "send"), None),
            P(("recv", "send"), None),
            P(("recv", "send")),
            P(("recv", "send")),
            P(("recv", "send")),
            P(("recv", "send"), None),
            P(),
            P(),
            P(),
            P(),
            P(),
        ),
        out_specs=(
            P(("recv", "send"), None),
            P(("recv", "send"), None),
            P(("recv", "send"), None),
            P(),
            P(),
            P(),
        ),
        check_vma=False,
    )
```
